128 devices in a mesh: lat: 8 (over z, core), lon: 16 (over x, y).
Axes of the slice: x: 4, y: 4, z: 4, core: 2. Of those that a mesh axis runs over, the one named last changes fastest.
Arguments:
- patches: bfloat16 [24576, 1536], P(('lat', 'lon')), may hold values from -6 to 6
- requests: int32 [8, 8192], P('lat', 'lon'), may hold values from 0 to 191, as said below
- footprint: int32 [512, 128], P('lat', 'lon'), may hold values from -1 to 511, as said below
- weight_index: int32 [512, 128], P('lat', 'lon'), may hold values from 0 to 15
- composite_weights: float32 [16], replicated, may hold values from 0.1 to 1
- labels: int32 [512, 2048], P('lat', 'lon'), may hold values from 0 to 10
- conv1_weight: bfloat16 [9, 64, 12], replicated, may hold values from -0.625 to 0.625
- conv2_weight: bfloat16 [9, 64, 64], replicated, may hold values from -0.25 to 0.25
- head_weight: bfloat16 [11, 64], replicated, may hold values from -0.75 to 0.75
Outputs:
- skip_features: bfloat16 [64, 512, 2048], P(None, 'lat', 'lon')
- grad_conv1: float32 [9, 64, 12], replicated
- grad_conv2: float32 [9, 64, 64], replicated
- grad_head: float32 [11, 64], replicated
- loss: float32 [], replicated
The draws below stay inside these ranges and needn't reach their ends.
Inputs may be any that keep to these rules, and one draw needn't show every extreme that they name: `requests`: every entry is a row offset into the store of the device at the same lat index and lon index b. `footprint`: an entry that is not -1 is b*32 + p, position p of the bucket that the tile takes from lon index b. Slot 0 is never -1. In one tile no two entries are equal, and in some tiles every position of every bucket is named.
All inputs are finite; a program needn't handle non-finite values.
Results may differ from the reference program's by a relative error of at most 0.0055.
Values may be sent and summed in bfloat16 or wider, within the bound.
A program may use at most 64 MiB of HBM per device.

```python
import math
import jax
import jax.numpy as jnp
from jax import lax

TILE_ROWS = 64
PATCH_PX = 128
BANDS = 12
FEAT = 64
NCLASS = 11
SLOTS = 8
TAPS = 9
QUALITY = 16
STORE_DEV = 192
BUCKET = 32
IMG_ROWS = 512
IMG_COLS = 2048
N_LAT = 8
N_LON = 16


def routing_plan(key):
    tile_count = N_LAT * N_LON
    keys = [jax.random.fold_in(key, 101 + number) for number in range(6)]
    draw_level = jax.random.randint(keys[0], (tile_count,), 0, 65)
    scene_count = 1 + (SLOTS - 1) * draw_level * (draw_level + 64) // (2 * 64 * 64)
    tile_ids = jnp.arange(tile_count, dtype=jnp.int32)
    forced = tile_ids % N_LON == tile_ids // N_LON % N_LON
    scene_count = jnp.where(forced, SLOTS, scene_count)
    lon_ids = jnp.arange(N_LON, dtype=jnp.int32)
    scores = jax.random.randint(keys[1], (tile_count, N_LON), 0, 1 << 20) * N_LON + lon_ids[None, :]
    owners = jnp.argsort(scores, axis=1).astype(jnp.int32)
    slot_ids = jnp.arange(SLOTS, dtype=jnp.int32)
    row_ids = jnp.arange(TILE_ROWS, dtype=jnp.int32)
    starts = jax.random.randint(keys[3], (tile_count, SLOTS), 0, TILE_ROWS // 5 + 1)
    starts = jnp.where(forced[:, None] | (slot_ids[None, :] == 0), 0, starts)
    order = slot_ids[None, :] * TILE_ROWS + row_ids[:, None]
    run_index = order // BUCKET
    position = order % BUCKET
    owner_of = owners[:, run_index]
    in_use = (slot_ids[None, None, :] < scene_count[:, None, None]) & (row_ids[None, :, None] >= starts[:, None, :])
    foot_value = jnp.where(in_use, owner_of * BUCKET + position[None], -1)
    footprint = foot_value.reshape(N_LAT, N_LON, TILE_ROWS, SLOTS).transpose(0, 2, 1, 3).reshape(N_LAT * TILE_ROWS, N_LON * SLOTS)
    shifts = jax.random.randint(keys[2], (tile_count, N_LON), 0, BUCKET)
    bases = jax.random.randint(keys[4], (tile_count, N_LON), 0, STORE_DEV - BUCKET + 1)
    bases = jnp.where(forced[:, None] & (lon_ids[None, :] == 0), STORE_DEV - BUCKET, bases)
    bases = jnp.where(forced[:, None] & (lon_ids[None, :] == 1), 0, bases)
    bucket_ids = jnp.arange(BUCKET, dtype=jnp.int32)
    requests = bases[:, :, None] + (bucket_ids[None, None, :] + shifts[:, :, None]) % BUCKET
    return (footprint.astype(jnp.int32), requests.reshape(N_LAT, N_LON * N_LON * BUCKET).astype(jnp.int32))


def draw_requests(key, part):
    return routing_plan(key)[1]


def draw_footprint(key, part):
    return routing_plan(key)[0]


def touch_ends(entries, stream_key, least, top_value):
    index_at = [jax.random.randint(jax.random.fold_in(stream_key, axis), (), 0, length) for axis, length in enumerate(entries.shape)]
    widest = entries.shape.index(max(entries.shape))
    neighbour = index_at[:widest] + [(index_at[widest] + 1) % entries.shape[widest]] + index_at[widest + 1:]
    return entries.at[tuple(index_at)].set(least).at[tuple(neighbour)].set(top_value)


def shard_levels(own_key, extent, cuts, low, largest):
    def one(dim, parts):
        heights = jax.random.uniform(jax.random.fold_in(jax.random.fold_in(own_key, 6), dim), (parts,), jnp.float32, low / len(cuts), largest / len(cuts))
        return jnp.repeat(jnp.exp(heights), extent[dim] // parts).reshape((-1,) + (1,) * (len(extent) - dim - 1))

    factor_of = one(*cuts[0])
    for cut in cuts[1:]:
        factor_of = factor_of * one(*cut)
    return factor_of


def noise(rng, shape, spread, reach, shards=(), kind=jnp.bfloat16):
    drawn = spread * jax.random.normal(rng, shape, jnp.float32)
    if shards:
        drawn = drawn * shard_levels(rng, shape, shards, -0.22, 0.18)
    return jnp.clip(drawn, -reach, reach).astype(kind)


def setup_inputs(seed: int = 0) -> dict:
    seeds = jax.random.split(jax.random.key(seed), 10)
    patches = noise(seeds[0], (N_LAT * N_LON * STORE_DEV, BANDS * PATCH_PX), 1.0, 6.0, ((0, 128),))
    requests = draw_requests(jax.random.fold_in(seeds[9], 71), 0)
    footprint = draw_footprint(jax.random.fold_in(seeds[9], 71), 0)
    weight_index = touch_ends(jax.random.randint(seeds[3], (IMG_ROWS, N_LON * SLOTS), 0, QUALITY), jax.random.fold_in(seeds[3], 1), 0, QUALITY - 1).astype(jnp.int32)
    composite_weights = jnp.clip(jnp.exp(jax.random.uniform(seeds[4], (QUALITY,), jnp.float32, math.log(0.1), math.log(1.0))), 0.1, 1.0)
    labels = touch_ends(jax.random.randint(seeds[5], (IMG_ROWS, IMG_COLS), 0, NCLASS), jax.random.fold_in(seeds[5], 1), 0, NCLASS - 1).astype(jnp.int32)
    conv1_weight = noise(seeds[6], (TAPS, FEAT, BANDS), (TAPS * BANDS) ** -0.5, 0.625)
    conv2_weight = noise(seeds[7], (TAPS, FEAT, FEAT), (TAPS * FEAT) ** -0.5, 0.25)
    head_weight = noise(seeds[8], (NCLASS, FEAT), FEAT ** -0.5, 0.75)
    return {"patches": patches, "requests": requests, "footprint": footprint, "weight_index": weight_index, "composite_weights": composite_weights, "labels": labels, "conv1_weight": conv1_weight, "conv2_weight": conv2_weight, "head_weight": head_weight}


def silu_slope(pre_value):
    sigmoid_value = jax.nn.sigmoid(pre_value)
    return sigmoid_value * (1.0 + pre_value * (1.0 - sigmoid_value))

def conv_forward(padded, weight, out_rows, out_cols):
    channels = padded.shape[0]
    result = jnp.zeros((weight.shape[1], out_rows * out_cols), jnp.float32)
    for tap_index in range(TAPS):
        tap_row, tap_col = (tap_index // 3, tap_index % 3)
        window = padded[:, tap_row:tap_row + out_rows, tap_col:tap_col + out_cols].reshape(channels, out_rows * out_cols)
        result = result + jnp.dot(weight[tap_index], window, preferred_element_type=jnp.float32)
    return result.reshape(weight.shape[1], out_rows, out_cols)

def conv_adjoint(padded, weight, out_rows, out_cols):
    channels = padded.shape[0]
    result = jnp.zeros((weight.shape[2], out_rows * out_cols), jnp.float32)
    for tap_index in range(TAPS):
        tap_row, tap_col = (2 - tap_index // 3, 2 - tap_index % 3)
        window = padded[:, tap_row:tap_row + out_rows, tap_col:tap_col + out_cols].reshape(channels, out_rows * out_cols)
        result = result + lax.dot_general(weight[tap_index], window, (((0,), (0,)), ((), ())), preferred_element_type=jnp.float32)
    return result.reshape(weight.shape[2], out_rows, out_cols)

def weight_grad(slope, padded, out_rows, out_cols):
    channels = padded.shape[0]
    slope_flat = slope.reshape(slope.shape[0], out_rows * out_cols)
    grads = []
    for tap_index in range(TAPS):
        tap_row, tap_col = (tap_index // 3, tap_index % 3)
        window = padded[:, tap_row:tap_row + out_rows, tap_col:tap_col + out_cols].reshape(channels, out_rows * out_cols)
        grads.append(lax.dot_general(slope_flat, window, (((1,), (1,)), ((), ())), preferred_element_type=jnp.float32))
    return jnp.stack(grads)

def reference(patches, requests, footprint, weight_index, composite_weights, labels, conv1_weight, conv2_weight, head_weight):
    row_width = BANDS * PATCH_PX
    slot_lon = jnp.arange(N_LON * SLOTS, dtype=jnp.int32) // SLOTS

    def composite_strip(inputs):
        strip_index, foot_rows, level_rows, asked_rows = inputs
        entry_index = jnp.maximum(foot_rows, 0)
        source = entry_index // BUCKET
        offset = asked_rows[((slot_lon[None, :] * N_LON + source) * BUCKET + entry_index % BUCKET).astype(jnp.int32)]
        global_row = ((strip_index * N_LON + source) * STORE_DEV + offset).astype(jnp.int32)
        gathered = patches[global_row.reshape(-1)].reshape(TILE_ROWS, N_LON, SLOTS, row_width)
        slot_scale = jnp.where(foot_rows >= 0, composite_weights[level_rows], 0.0).reshape(TILE_ROWS, N_LON, SLOTS)
        blended = lax.optimization_barrier(jnp.sum(slot_scale[..., None] * gathered.astype(jnp.float32), axis=2))
        blended = blended / lax.optimization_barrier(jnp.sum(slot_scale, axis=2))[..., None]
        blended = blended.astype(jnp.bfloat16).reshape(TILE_ROWS, N_LON, BANDS, PATCH_PX)
        return blended.transpose(2, 0, 1, 3).reshape(BANDS, TILE_ROWS, IMG_COLS)
    strips = lax.map(composite_strip, (jnp.arange(N_LAT, dtype=jnp.int32), footprint.reshape(N_LAT, TILE_ROWS, N_LON * SLOTS), weight_index.reshape(N_LAT, TILE_ROWS, N_LON * SLOTS), requests))
    composite = strips.transpose(1, 0, 2, 3).reshape(BANDS, IMG_ROWS, IMG_COLS)
    band_pad = jnp.pad(composite, ((0, 0), (1, 1), (1, 1)))
    pre_one = conv_forward(band_pad, conv1_weight, IMG_ROWS, IMG_COLS)
    hidden_one = jax.nn.silu(pre_one).astype(jnp.bfloat16)
    hidden_pad = jnp.pad(hidden_one, ((0, 0), (1, 1), (1, 1)))
    pre_two = conv_forward(hidden_pad, conv2_weight, IMG_ROWS, IMG_COLS)
    skip_features = jax.nn.silu(pre_two).astype(jnp.bfloat16)
    skip_flat = skip_features.reshape(FEAT, IMG_ROWS * IMG_COLS)
    logits = jnp.dot(head_weight, skip_flat, preferred_element_type=jnp.float32)
    log_total = jnp.log(lax.optimization_barrier(jnp.sum(jnp.exp(logits), axis=0)))
    onehot = labels.reshape(-1)[None, :] == jnp.arange(NCLASS, dtype=jnp.int32)[:, None]
    loss_sum = jnp.sum(log_total - lax.optimization_barrier(jnp.sum(jnp.where(onehot, logits, 0.0), axis=0)))
    class_error = (jnp.exp(logits - log_total[None, :]) - onehot.astype(jnp.float32)).astype(jnp.bfloat16)
    grad_head = lax.dot_general(class_error, skip_flat, (((1,), (1,)), ((), ())), preferred_element_type=jnp.float32)
    back_two = lax.dot_general(head_weight, class_error, (((0,), (0,)), ((), ())), preferred_element_type=jnp.float32)
    slope_two = (back_two.reshape(FEAT, IMG_ROWS, IMG_COLS) * silu_slope(pre_two)).astype(jnp.bfloat16)
    grad_two = weight_grad(slope_two, hidden_pad, IMG_ROWS, IMG_COLS)
    slope_pad = jnp.pad(slope_two, ((0, 0), (1, 1), (1, 1)))
    back_one = conv_adjoint(slope_pad, conv2_weight, IMG_ROWS, IMG_COLS)
    slope_one = (back_one * silu_slope(pre_one)).astype(jnp.bfloat16)
    grad_one = weight_grad(slope_one, band_pad, IMG_ROWS, IMG_COLS)
    pixel_count = IMG_ROWS * IMG_COLS
    return (skip_features, grad_one / pixel_count, grad_two / pixel_count, grad_head / pixel_count, loss_sum / pixel_count)
```

```python
import functools

import jax
import jax.numpy as jnp
from jax import lax
from jax.experimental import pallas as pl
from jax.experimental.pallas import tpu as pltpu
from jax.sharding import PartitionSpec as P

F32 = jnp.float32
BF16 = jnp.bfloat16
NLAT, NLON = 8, 16
ROWS, COLS, BANDS, FEAT, NCLASS, SLOTS, BUCKET, STORE = 64, 128, 12, 64, 11, 8, 32, 192
WIDTH = BANDS * COLS
CHUNKS = 3
CW = WIDTH // CHUNKS
MESH = pl.DeviceIdType.MESH
VM = pl.BlockSpec(memory_space=pltpu.VMEM)


def lane_iota(shape):
    return lax.broadcasted_iota(jnp.int32, shape, len(shape) - 1)


def dot_nt(a, b):
    return lax.dot_general(a, b, (((1,), (1,)), ((), ())), preferred_element_type=F32)


def dot_tn(a, b):
    return lax.dot_general(a, b, (((0,), (0,)), ((), ())), preferred_element_type=F32)


def dot(a, b):
    return jnp.dot(a, b, preferred_element_type=F32)


def gather_kernel(
    patches, requests, foot, widx, cw, labels, comp, strip,
    reqs, hot, sendbuf, recv, bands, picked, hsend, from_up, from_down, side,
    req_send, req_recv, row_send, row_recv, halo_send, halo_recv,
):
    lat, lon = lax.axis_index("lat"), lax.axis_index("lon")
    up, down = lax.rem(lat + NLAT - 1, NLAT), lax.rem(lat + 1, NLAT)
    left, right = lax.rem(lon + NLON - 1, NLON), lax.rem(lon + 1, NLON)

    barrier = pltpu.get_barrier_semaphore()

    def greet(k, _):
        peer = lax.rem(lon + k, NLON)
        pl.semaphore_signal(barrier, inc=1, device_id=(lat, peer), device_id_type=MESH)
        return 0

    lax.fori_loop(1, NLON, greet, 0)
    for i in (up, down):
        for d in (left, lon, right):
            pl.semaphore_signal(barrier, inc=1, device_id=(i, d), device_id_type=MESH)
    pl.semaphore_wait(barrier, NLON - 1 + 6)

    def req_copy(k, peer):
        start = pl.multiple_of((peer // 4) * 128, 128)
        return pltpu.make_async_remote_copy(
            src_ref=requests.at[:, pl.ds(start, 128)], dst_ref=reqs.at[lon],
            send_sem=req_send.at[k], recv_sem=req_recv.at[lon],
            device_id=(lat, peer), device_id_type=MESH)

    def req_arrival(source):
        return pltpu.make_async_remote_copy(
            src_ref=requests.at[:, pl.ds(0, 128)], dst_ref=reqs.at[source],
            send_sem=req_send.at[0], recv_sem=req_recv.at[source],
            device_id=(lat, lon), device_id_type=MESH)

    def send_req(k, _):
        req_copy(k, lax.rem(lon + k, NLON)).start()
        return 0

    lax.fori_loop(1, NLON, send_req, 0)
    own = pl.multiple_of((lon // 4) * 128, 128)
    reqs[lon] = requests[:, pl.ds(own, 128)]

    level = widx[...]
    weight = jnp.zeros((ROWS, SLOTS), F32)
    for q in range(16):
        weight = jnp.where(level == q, cw[q], weight)
    entry = foot[...]
    weight = jnp.where(entry >= 0, weight, 0.0)
    total = jnp.sum(weight, axis=1, keepdims=True)
    position = lane_iota((ROWS, NLON * BUCKET))
    blend = jnp.zeros((ROWS, NLON * BUCKET), F32)
    for k in range(SLOTS):
        blend = blend + jnp.where(entry[:, k : k + 1] == position, weight[:, k : k + 1], 0.0)
    blend_hi = blend.astype(BF16)
    blend_lo = (blend - blend_hi.astype(F32)).astype(BF16)

    def wait_req(k, _):
        req_arrival(lax.rem(lon + k, NLON)).wait_recv()
        return 0

    lax.fori_loop(1, NLON, wait_req, 0)

    lanes = lane_iota((1, 128))
    base = 32 * lax.rem(lon, 4)
    store_row = lax.broadcasted_iota(jnp.int32, (STORE, 128), 0)
    for t in range(4):
        asked = jnp.zeros((1, 128), jnp.int32)
        for j in range(4):
            turned = pltpu.roll(reqs[4 * t + j], lax.rem(32 * j - base + 128, 128), 1)
            asked = jnp.where((lanes >= 32 * j) & (lanes < 32 * j + 32), turned, asked)
        hot[:, 128 * t : 128 * (t + 1)] = jnp.where(store_row == asked, 1.0, 0.0).astype(BF16)

    def row_copy(c, k, peer):
        return pltpu.make_async_remote_copy(
            src_ref=sendbuf.at[c, peer], dst_ref=recv.at[c, lon],
            send_sem=row_send.at[c, k], recv_sem=row_recv.at[c, lon],
            device_id=(lat, peer), device_id_type=MESH)

    def row_arrival(c, source):
        return pltpu.make_async_remote_copy(
            src_ref=sendbuf.at[c, source], dst_ref=recv.at[c, source],
            send_sem=row_send.at[c, 0], recv_sem=row_recv.at[c, source],
            device_id=(lat, lon), device_id_type=MESH)

    for c in range(CHUNKS):
        rows = dot_tn(hot[...], patches[:, c * CW : (c + 1) * CW]).astype(BF16)
        sendbuf[c] = rows.reshape(NLON, BUCKET, CW)

        def send_rows(k, _):
            row_copy(c, k, lax.rem(lon + k, NLON)).start()
            return 0

        lax.fori_loop(1, NLON, send_rows, 0)
        recv[c, lon] = sendbuf[c, lon]

    for k in range(BANDS + 1, 16):
        bands[k] = jnp.zeros((ROWS, COLS), F32)
    bands[BANDS] = labels[...].astype(F32)
    for c in range(CHUNKS):

        def wait_rows(k, _):
            row_arrival(c, lax.rem(lon + k, NLON)).wait_recv()
            return 0

        lax.fori_loop(1, NLON, wait_rows, 0)
        rows = recv[c].reshape(NLON * BUCKET, CW)
        blended = (dot(blend_hi, rows) + dot(blend_lo, rows)) / total
        blended = blended.astype(BF16).astype(F32)
        for b in range(CW // COLS):
            bands[c * (CW // COLS) + b] = blended[:, b * COLS : (b + 1) * COLS]

    pick_row = lax.broadcasted_iota(jnp.int32, (8, COLS), 0)
    pick_lane = lane_iota((8, COLS))
    pick = jnp.where(pick_lane == jnp.where(pick_row < 3, pick_row, pick_row + 122), 1.0, 0.0)
    columns = dot_nt(pick.astype(BF16), bands[...].reshape(16 * ROWS, COLS).astype(BF16))
    for k in range(16):
        picked[k] = jnp.concatenate(
            [columns[:, k * ROWS : (k + 1) * ROWS], jnp.zeros((8, 64), F32)], axis=1)
    for x in range(3):
        hsend[3 + x] = picked[:, x, :].astype(BF16)
        hsend[6 + x] = picked[:, 3 + x, :].astype(BF16)
    for r in range(3):
        hsend[r] = bands[:, r, :].astype(BF16)
        hsend[9 + r] = bands[:, ROWS - 3 + r, :].astype(BF16)

    def halo_copies():
        made = [
            (hsend.at[0:9], from_down, (up, lon)),
            (hsend.at[3:12], from_up, (down, lon)),
            (hsend.at[3:6], side.at[3], (lat, left)),
            (hsend.at[6:9], side.at[0], (lat, right)),
            (hsend.at[3:6], side.at[5], (up, left)),
            (hsend.at[6:9], side.at[2], (up, right)),
            (hsend.at[3:6], side.at[4], (down, left)),
            (hsend.at[6:9], side.at[1], (down, right)),
        ]
        return [
            pltpu.make_async_remote_copy(
                src_ref=s, dst_ref=d, send_sem=halo_send.at[n], recv_sem=halo_recv.at[n],
                device_id=who, device_id_type=MESH)
            for n, (s, d, who) in enumerate(made)
        ]

    copies = halo_copies()
    for copy in copies:
        copy.start()

    for r in range(ROWS):
        comp[3 + r] = bands[:, r, :].astype(BF16)

    for copy in copies:
        copy.wait_recv()

    has_up, has_down = lat > 0, lat < NLAT - 1
    has_left, has_right = lon > 0, lon < NLON - 1
    for r in range(3):
        comp[r] = jnp.where(has_up, from_up[6 + r].astype(F32), 0.0).astype(BF16)
        comp[67 + r] = jnp.where(has_down, from_down[r].astype(F32), 0.0).astype(BF16)
    tile_lane = lane_iota((16, 128))

    def joined(middle, above, below, inside):
        turned = pltpu.roll(middle.astype(F32), 3, 1)
        result = jnp.where((tile_lane >= 3) & (tile_lane < 67), turned, 0.0)
        top = pltpu.roll(above.astype(F32), 67, 1)
        result = jnp.where((tile_lane < 3) & has_up, top, result)
        bottom = pltpu.roll(below.astype(F32), 67, 1)
        result = jnp.where((tile_lane >= 67) & (tile_lane < 70) & has_down, bottom, result)
        if inside is not None:
            result = jnp.where(inside, result, 0.0)
        return result.astype(BF16)

    for x in range(3):
        strip[x] = joined(side[0, x], side[1, x], side[2, x], has_left)
        strip[7 + x] = joined(side[3, x], side[4, x], side[5, x], has_right)
    for x in range(2):
        strip[3 + x] = joined(hsend[3 + x], from_up[x], from_down[3 + x], None)
        strip[5 + x] = joined(hsend[7 + x], from_up[4 + x], from_down[7 + x], None)

    for copy in copies:
        copy.wait_send()

    def drain(k, _):
        peer = lax.rem(lon + k, NLON)
        req_copy(k, peer).wait_send()
        for c in range(CHUNKS):
            row_copy(c, k, peer).wait_send()
        return 0

    lax.fori_loop(1, NLON, drain, 0)


def gather(patches, requests, foot, widx, cw, labels):
    return pl.pallas_call(
        gather_kernel,
        out_shape=(
            jax.ShapeDtypeStruct((70, 16, 128), BF16),
            jax.ShapeDtypeStruct((10, 16, 128), BF16),
        ),
        in_specs=[VM, VM, VM, VM, pl.BlockSpec(memory_space=pltpu.SMEM), VM],
        out_specs=(VM, VM),
        scratch_shapes=[
            pltpu.VMEM((NLON, 1, 128), jnp.int32),
            pltpu.VMEM((STORE, NLON * BUCKET), BF16),
            pltpu.VMEM((CHUNKS, NLON, BUCKET, CW), BF16),
            pltpu.VMEM((CHUNKS, NLON, BUCKET, CW), BF16),
            pltpu.VMEM((16, ROWS, COLS), F32),
            pltpu.VMEM((16, 8, 128), F32),
            pltpu.VMEM((12, 16, 128), BF16),
            pltpu.VMEM((9, 16, 128), BF16),
            pltpu.VMEM((9, 16, 128), BF16),
            pltpu.VMEM((6, 3, 16, 128), BF16),
            pltpu.SemaphoreType.DMA((NLON,)),
            pltpu.SemaphoreType.DMA((NLON,)),
            pltpu.SemaphoreType.DMA((CHUNKS, NLON)),
            pltpu.SemaphoreType.DMA((CHUNKS, NLON)),
            pltpu.SemaphoreType.DMA((8,)),
            pltpu.SemaphoreType.DMA((8,)),
        ],
        compiler_params=pltpu.CompilerParams(collective_id=0, has_side_effects=True),
        name="gather_blend_halo",
    )(patches, requests, foot, widx, cw, labels)


def sigmoid(v):
    return 0.5 * jnp.tanh(0.5 * v) + 0.5


def slope_of(v, s):
    return s * (1.0 + v * (1.0 - s))


def tile_kernel(
    comp, strip, w1, w2, head, skip_out, grads,
    w1k, w2k, w2a, x1, x2, x3, pre1, sk, edge, hid, skip3, acc2, acc1, acch, accl,
):
    lat, lon = lax.axis_index("lat"), lax.axis_index("lon")
    has_up, has_down = lat > 0, lat < NLAT - 1
    has_left, has_right = lon > 0, lon < NLON - 1

    w1k[...] = jnp.zeros_like(w1k)
    for t in range(9):
        w1k[:, 16 * t : 16 * t + BANDS] = w1[t]
        w2k[:, 64 * t : 64 * (t + 1)] = w2[t]
        w2a[:, 64 * t : 64 * (t + 1)] = w2[8 - t].astype(F32).T.astype(BF16)
    headp = jnp.concatenate(
        [head[...].astype(F32), jnp.zeros((16 - NCLASS, FEAT), F32)], axis=0).astype(BF16)

    def spread(dst, tile, index, tile_f32, left_col, right_col, lane_row, height):
        lanes = lane_iota((height, 128))
        put_left = pltpu.roll(left_col, lax.rem(128 - lane_row, 128), 1)
        put_right = pltpu.roll(right_col, lax.rem(255 - lane_row, 128), 1)
        at = pl.ds(pl.multiple_of(index * 128, 128), 128)
        dst[0:height, at] = jnp.where(lanes == 0, put_left, pltpu.roll(tile_f32, 1, 1)).astype(BF16)
        dst[height : 2 * height, at] = tile
        dst[2 * height : 3 * height, at] = jnp.where(
            lanes == 127, put_right, pltpu.roll(tile_f32, 127, 1)).astype(BF16)

    comp_left = strip[2].astype(F32)
    comp_right = strip[7].astype(F32)

    def spread_comp(i, _):
        for j in range(7):
            t = i * 7 + j
            tile = comp[t]
            spread(x1, tile, t, tile.astype(F32), comp_left, comp_right, t, 16)
        return 0

    lax.fori_loop(0, 10, spread_comp, 0)

    lanes16 = lane_iota((16, 128))
    del lanes16
    turned = [[pltpu.roll(strip[s].astype(F32), (128 - u) % 128, 1).astype(BF16) for u in (-1, 0, 1)]
              for s in range(10)]
    lanes64 = lane_iota((FEAT, 128))
    row_ok = ((lanes64 >= 3) | has_up) & ((lanes64 < 67) | has_down) & (lanes64 >= 1) & (lanes64 < 69)
    for n, s in enumerate((1, 2, 3, 6, 7, 8)):
        stack = jnp.concatenate([turned[s + v][u] for u in range(3) for v in (-1, 0, 1)], axis=0)
        pre = dot(w1k[...], stack)
        keep = row_ok
        if s in (1, 2):
            keep = keep & has_left
        if s in (7, 8):
            keep = keep & has_right
        hid[n] = jnp.where(keep, pre * sigmoid(pre), 0.0)
    hid_left = hid[1]
    hid_right = hid[4]

    def stack_of(ref, first, count):
        return jnp.concatenate(
            [ref[:, pl.ds(pl.multiple_of((first + u) * 128, 128), count * 128)] for u in (-1, 0, 1)],
            axis=0)

    for first, inside in ((1, has_up), (67, has_down)):
        pre = dot(w1k[...], stack_of(x1, first, 2))
        value = jnp.where(inside, pre * sigmoid(pre), 0.0)
        for j in range(2):
            tile = value[:, 128 * j : 128 * (j + 1)]
            spread(x2, tile.astype(BF16), first - 1 + j, tile, hid_left, hid_right, first + j, FEAT)

    def conv_one(i, _):
        first = i * 8
        pre = dot(w1k[...], stack_of(x1, first + 3, 8))
        pre1[:, pl.ds(pl.multiple_of(first * 128, 128), 1024)] = pre
        value = pre * sigmoid(pre)
        for j in range(8):
            tile = value[:, 128 * j : 128 * (j + 1)]
            spread(x2, tile.astype(BF16), first + 2 + j, tile, hid_left, hid_right, first + 3 + j, FEAT)
        return 0

    lax.fori_loop(0, 8, conv_one, 0)

    def head_of(pre, label):
        width = pre.shape[1]
        s = sigmoid(pre)
        skip = (pre * s).astype(BF16)
        logits = dot(headp, skip)
        classes = lax.broadcasted_iota(jnp.int32, (16, width), 0)
        power = jnp.where(classes < NCLASS, jnp.exp(logits), 0.0)
        total = jnp.sum(power, axis=0, keepdims=True)
        onehot = classes == label.astype(jnp.int32)
        error = (power / total - jnp.where(onehot, 1.0, 0.0)).astype(BF16)
        slope = dot_tn(headp, error) * slope_of(pre, s)
        loss = jnp.log(total) - jnp.sum(jnp.where(onehot, logits, 0.0), axis=0, keepdims=True)
        return skip, error, slope, loss

    edge[:, 0:128] = dot(w2k[...], stack_of(x2, 1, 1))
    edge[:, 128:256] = dot(w2k[...], stack_of(x2, 66, 1))
    for n, middle in enumerate((1, 4)):
        stack = jnp.concatenate(
            [pltpu.roll(hid[middle + v], (128 - u) % 128, 1).astype(BF16)
             for u in (-1, 0, 1) for v in (-1, 0, 1)], axis=0)
        edge[:, 256 + 128 * n : 384 + 128 * n] = dot(w2k[...], stack)

    def label_row(tile):
        return tile.astype(F32)[BANDS : BANDS + 1, :]

    edge_label = jnp.concatenate(
        [label_row(comp[2]), label_row(comp[67]), label_row(strip[2]), label_row(strip[7])], axis=1)
    _, _, edge_slope, _ = head_of(edge[...], edge_label)
    slope_left = jnp.where(row_ok & has_left, edge_slope[:, 256:384], 0.0)
    slope_right = jnp.where(row_ok & has_right, edge_slope[:, 384:512], 0.0)
    slope_top = jnp.where(has_up, edge_slope[:, 0:128], 0.0)
    slope_bottom = jnp.where(has_down, edge_slope[:, 128:256], 0.0)
    hid[0] = slope_left
    hid[2] = slope_right
    spread(x3, slope_top.astype(BF16), 0, slope_top, slope_left, slope_right, 2, FEAT)
    spread(x3, slope_bottom.astype(BF16), 65, slope_bottom, slope_left, slope_right, 67, FEAT)

    acc2[...] = jnp.zeros_like(acc2)
    acc1[...] = jnp.zeros_like(acc1)
    acch[...] = jnp.zeros_like(acch)
    accl[...] = jnp.zeros_like(accl)

    def conv_two(i, _):
        first = i * 8
        stack = stack_of(x2, first + 2, 8)
        pre = dot(w2k[...], stack)
        label = jnp.concatenate([label_row(comp[first + 3 + j]) for j in range(8)], axis=1)
        skip, error, slope, loss = head_of(pre, label)
        acch[...] += dot_nt(skip, error)
        accl[...] += loss
        skip_f32 = skip.astype(F32)
        left_col, right_col = hid[0], hid[2]
        for j in range(8):
            tile = slope[:, 128 * j : 128 * (j + 1)]
            spread(x3, tile.astype(BF16), first + 1 + j, tile, left_col, right_col, first + 3 + j, FEAT)
            skip3[:, j, :] = skip_f32[:, 128 * j : 128 * (j + 1)]
        skip_out[:, pl.ds(pl.multiple_of(first, 8), 8), :] = skip3[...].astype(BF16)
        acc2[...] += dot_nt(slope.astype(BF16), stack)
        return 0

    lax.fori_loop(0, 8, conv_two, 0)

    def back_one(i, _):
        first = i * 8
        back = dot(w2a[...], stack_of(x3, first + 1, 8))
        pre = pre1[:, pl.ds(pl.multiple_of(first * 128, 128), 1024)]
        slope = (back * slope_of(pre, sigmoid(pre))).astype(BF16)
        acc1[...] += dot_nt(slope, stack_of(x1, first + 3, 8))
        return 0

    lax.fori_loop(0, 8, back_one, 0)

    loss_total = jnp.sum(jnp.sum(accl[...], axis=1, keepdims=True), axis=0, keepdims=True)
    packed = jnp.concatenate(
        [acc2[...], acc1[...], acch[...], jnp.broadcast_to(loss_total, (FEAT, 32))], axis=1)
    for g in range(8):
        for h in range(6):
            grads[6 * g + h] = packed[8 * g : 8 * (g + 1), 128 * h : 128 * (h + 1)]


def tile_pass(comp, strip, w1, w2, head):
    return pl.pallas_call(
        tile_kernel,
        out_shape=(
            jax.ShapeDtypeStruct((FEAT, ROWS, COLS), BF16),
            jax.ShapeDtypeStruct((48, 8, 128), F32),
        ),
        in_specs=[VM] * 5,
        out_specs=(VM, VM),
        scratch_shapes=[
            pltpu.VMEM((64, 144), BF16),
            pltpu.VMEM((64, 576), BF16),
            pltpu.VMEM((64, 576), BF16),
            pltpu.VMEM((48, 70 * 128), BF16),
            pltpu.VMEM((192, 68 * 128), BF16),
            pltpu.VMEM((192, 66 * 128), BF16),
            pltpu.VMEM((64, 64 * 128), F32),
            pltpu.VMEM((8, 128), F32),
            pltpu.VMEM((64, 512), F32),
            pltpu.VMEM((6, 64, 128), F32),
            pltpu.VMEM((64, 8, 128), F32),
            pltpu.VMEM((64, 576), F32),
            pltpu.VMEM((64, 144), F32),
            pltpu.VMEM((64, 16), F32),
            pltpu.VMEM((1, 1024), F32),
        ],
        name="tile_forward_backward",
    )(comp, strip, w1, w2, head)


def sum_kernel(part, out, first, second, whole, s1, r1, s2, r2, s3, r3):
    lat, lon = lax.axis_index("lat"), lax.axis_index("lon")
    barrier = pltpu.get_barrier_semaphore()

    def greet_lon(k, _):
        pl.semaphore_signal(
            barrier, inc=1, device_id=(lat, lax.rem(lon + k, NLON)), device_id_type=MESH)
        return 0

    def greet_lat(k, _):
        pl.semaphore_signal(
            barrier, inc=1, device_id=(lax.rem(lat + k, NLAT), lon), device_id_type=MESH)
        return 0

    lax.fori_loop(1, NLON, greet_lon, 0)
    lax.fori_loop(1, NLAT, greet_lat, 0)
    pl.semaphore_wait(barrier, NLON - 1 + NLAT - 1)

    def scatter(k, peer, source):
        return pltpu.make_async_remote_copy(
            src_ref=part.at[pl.ds(3 * peer, 3)], dst_ref=first.at[source],
            send_sem=s1.at[k], recv_sem=r1.at[source],
            device_id=(lat, peer), device_id_type=MESH)

    def start1(k, _):
        scatter(k, lax.rem(lon + k, NLON), lon).start()
        return 0

    def wait1(k, _):
        peer = lax.rem(lon + k, NLON)
        scatter(k, peer, peer).wait_recv()
        return 0

    lax.fori_loop(1, NLON, start1, 0)
    first[lon] = part[pl.ds(3 * lon, 3)]
    lax.fori_loop(1, NLON, wait1, 0)
    piece = first[0]
    for n in range(1, NLON):
        piece = piece + first[n]
    second[lat] = piece

    def exchange(k, peer, source):
        return pltpu.make_async_remote_copy(
            src_ref=second.at[lat], dst_ref=second.at[source],
            send_sem=s2.at[k], recv_sem=r2.at[source],
            device_id=(peer, lon), device_id_type=MESH)

    def start2(k, _):
        exchange(k, lax.rem(lat + k, NLAT), lat).start()
        return 0

    def wait2(k, _):
        peer = lax.rem(lat + k, NLAT)
        exchange(k, peer, peer).wait_recv()
        return 0

    lax.fori_loop(1, NLAT, start2, 0)
    lax.fori_loop(1, NLAT, wait2, 0)
    piece = second[0]
    for n in range(1, NLAT):
        piece = piece + second[n]
    whole[pl.ds(3 * lon, 3)] = piece * (1.0 / (512 * 2048))

    def spread(k, peer, source):
        return pltpu.make_async_remote_copy(
            src_ref=whole.at[pl.ds(3 * lon, 3)], dst_ref=whole.at[pl.ds(3 * source, 3)],
            send_sem=s3.at[k], recv_sem=r3.at[source],
            device_id=(lat, peer), device_id_type=MESH)

    def start3(k, _):
        spread(k, lax.rem(lon + k, NLON), lon).start()
        return 0

    def wait3(k, _):
        peer = lax.rem(lon + k, NLON)
        spread(k, peer, peer).wait_recv()
        return 0

    lax.fori_loop(1, NLON, start3, 0)
    lax.fori_loop(1, NLON, wait3, 0)
    out[...] = whole[...]

    def drain(k, _):
        scatter(k, lax.rem(lon + k, NLON), lon).wait_send()
        spread(k, lax.rem(lon + k, NLON), lon).wait_send()
        return 0

    def drain2(k, _):
        exchange(k, lax.rem(lat + k, NLAT), lat).wait_send()
        return 0

    lax.fori_loop(1, NLON, drain, 0)
    lax.fori_loop(1, NLAT, drain2, 0)


def summed(part):
    return pl.pallas_call(
        sum_kernel,
        out_shape=jax.ShapeDtypeStruct((48, 8, 128), F32),
        in_specs=[VM],
        out_specs=VM,
        scratch_shapes=[
            pltpu.VMEM((NLON, 3, 8, 128), F32),
            pltpu.VMEM((NLAT, 3, 8, 128), F32),
            pltpu.VMEM((48, 8, 128), F32),
            pltpu.SemaphoreType.DMA((NLON,)),
            pltpu.SemaphoreType.DMA((NLON,)),
            pltpu.SemaphoreType.DMA((NLAT,)),
            pltpu.SemaphoreType.DMA((NLAT,)),
            pltpu.SemaphoreType.DMA((NLON,)),
            pltpu.SemaphoreType.DMA((NLON,)),
        ],
        compiler_params=pltpu.CompilerParams(collective_id=1, has_side_effects=True),
        name="gradient_sum",
    )(part)


def unpack_kernel(whole, grad1, grad2, gradh, loss):
    packed = jnp.concatenate(
        [jnp.concatenate([whole[6 * g + h] for h in range(6)], axis=1) for g in range(8)], axis=0)
    for t in range(9):
        grad2[t] = packed[:, 64 * t : 64 * (t + 1)]
        grad1[t] = packed[:, 576 + 16 * t : 576 + 16 * t + BANDS]
    gradh[...] = packed[:, 640:768].T[80 : 80 + NCLASS, :]
    loss[...] = packed[0:1, 736:737]


def unpacked(whole):
    return pl.pallas_call(
        unpack_kernel,
        out_shape=(
            jax.ShapeDtypeStruct((9, FEAT, BANDS), F32),
            jax.ShapeDtypeStruct((9, FEAT, FEAT), F32),
            jax.ShapeDtypeStruct((NCLASS, FEAT), F32),
            jax.ShapeDtypeStruct((1, 1), F32),
        ),
        in_specs=[VM],
        out_specs=(VM, VM, VM, VM),
        name="unpack",
    )(whole)


def body(patches, requests, foot, widx, cw, labels, w1, w2, head):
    comp, strip = gather(patches, requests, foot, widx, cw, labels)
    skip, part = tile_pass(comp, strip, w1, w2, head)
    grad1, grad2, gradh, loss = unpacked(summed(part))
    return skip, grad1, grad2, gradh, loss.reshape(())


def solution(mesh):
    placed = (
        P(("lat", "lon"), None),
        P("lat", "lon"),
        P("lat", "lon"),
        P("lat", "lon"),
        P(),
        P("lat", "lon"),
        P(),
        P(),
        P(),
    )
    return jax.shard_map(
        body,
        mesh=mesh,
        in_specs=placed,
        out_specs=(P(None, "lat", "lon"), P(), P(), P(), P()),
        check_vma=False,
    )
```

```python
import functools

import jax
import jax.numpy as jnp
from jax import lax
from jax.experimental import pallas as pl
from jax.experimental.pallas import tpu as pltpu
from jax.sharding import PartitionSpec as P

F32 = jnp.float32
BF16 = jnp.bfloat16
NLAT, NLON = 8, 16
ROWS, COLS, BANDS, FEAT, NCLASS, SLOTS, BUCKET, STORE = 64, 128, 12, 64, 11, 8, 32, 192
WIDTH = BANDS * COLS
CHUNKS = 3
CW = WIDTH // CHUNKS
MESH = pl.DeviceIdType.MESH
VM = pl.BlockSpec(memory_space=pltpu.VMEM)


def lane_iota(shape):
    return lax.broadcasted_iota(jnp.int32, shape, len(shape) - 1)


def dot_nt(a, b):
    return lax.dot_general(a, b, (((1,), (1,)), ((), ())), preferred_element_type=F32)


def dot_tn(a, b):
    return lax.dot_general(a, b, (((0,), (0,)), ((), ())), preferred_element_type=F32)


def dot(a, b):
    return jnp.dot(a, b, preferred_element_type=F32)


def gather_kernel(
    patches, requests, foot, widx, cw, labels, comp, strip,
    reqs, hot, sendbuf, recv, bands, picked, hsend, from_up, from_down, side,
    req_send, req_recv, row_send, row_recv, halo_send, halo_recv,
):
    lat, lon = lax.axis_index("lat"), lax.axis_index("lon")
    up, down = lax.rem(lat + NLAT - 1, NLAT), lax.rem(lat + 1, NLAT)
    left, right = lax.rem(lon + NLON - 1, NLON), lax.rem(lon + 1, NLON)

    barrier = pltpu.get_barrier_semaphore()

    def greet(k, _):
        peer = lax.rem(lon + k, NLON)
        pl.semaphore_signal(barrier, inc=1, device_id=(lat, peer), device_id_type=MESH)
        return 0

    lax.fori_loop(1, NLON, greet, 0)
    for i in (up, down):
        for d in (left, lon, right):
            pl.semaphore_signal(barrier, inc=1, device_id=(i, d), device_id_type=MESH)
    pl.semaphore_wait(barrier, NLON - 1 + 6)

    def req_copy(k, peer):
        start = pl.multiple_of((peer // 4) * 128, 128)
        return pltpu.make_async_remote_copy(
            src_ref=requests.at[:, pl.ds(start, 128)], dst_ref=reqs.at[lon],
            send_sem=req_send.at[k], recv_sem=req_recv.at[lon],
            device_id=(lat, peer), device_id_type=MESH)

    def req_arrival(source):
        return pltpu.make_async_remote_copy(
            src_ref=requests.at[:, pl.ds(0, 128)], dst_ref=reqs.at[source],
            send_sem=req_send.at[0], recv_sem=req_recv.at[source],
            device_id=(lat, lon), device_id_type=MESH)

    def send_req(k, _):
        req_copy(k, lax.rem(lon + k, NLON)).start()
        return 0

    lax.fori_loop(1, NLON, send_req, 0)
    own = pl.multiple_of((lon // 4) * 128, 128)
    reqs[lon] = requests[:, pl.ds(own, 128)]

    level = widx[...].astype(F32).T
    weight = jnp.zeros((ROWS, SLOTS), F32)
    for q in range(16):
        weight = jnp.where(level == q, cw[q], weight)
    entry = foot[...].astype(F32).T.astype(jnp.int32)
    weight = jnp.where(entry >= 0, weight, 0.0)
    total = jnp.sum(weight, axis=1, keepdims=True)
    position = lane_iota((ROWS, NLON * BUCKET))
    blend = jnp.zeros((ROWS, NLON * BUCKET), F32)
    for k in range(SLOTS):
        blend = blend + jnp.where(entry[:, k : k + 1] == position, weight[:, k : k + 1], 0.0)
    blend_hi = blend.astype(BF16)
    blend_lo = (blend - blend_hi.astype(F32)).astype(BF16)

    def wait_req(k, _):
        req_arrival(lax.rem(lon + k, NLON)).wait_recv()
        return 0

    lax.fori_loop(1, NLON, wait_req, 0)

    lanes = lane_iota((1, 128))
    base = 32 * lax.rem(lon, 4)
    store_row = lax.broadcasted_iota(jnp.int32, (STORE, 128), 0)
    for t in range(4):
        asked = jnp.zeros((1, 128), jnp.int32)
        for j in range(4):
            turned = pltpu.roll(reqs[4 * t + j], lax.rem(32 * j - base + 128, 128), 1)
            asked = jnp.where((lanes >= 32 * j) & (lanes < 32 * j + 32), turned, asked)
        hot[:, 128 * t : 128 * (t + 1)] = jnp.where(store_row == asked, 1.0, 0.0).astype(BF16)

    def row_copy(c, k, peer):
        return pltpu.make_async_remote_copy(
            src_ref=sendbuf.at[c, peer], dst_ref=recv.at[c, lon],
            send_sem=row_send.at[c, k], recv_sem=row_recv.at[c, lon],
            device_id=(lat, peer), device_id_type=MESH)

    def row_arrival(c, source):
        return pltpu.make_async_remote_copy(
            src_ref=sendbuf.at[c, source], dst_ref=recv.at[c, source],
            send_sem=row_send.at[c, 0], recv_sem=row_recv.at[c, source],
            device_id=(lat, lon), device_id_type=MESH)

    for c in range(CHUNKS):
        rows = dot_tn(hot[...], patches[:, c * CW : (c + 1) * CW]).astype(BF16)
        sendbuf[c] = rows.reshape(NLON, BUCKET, CW)

        def send_rows(k, _):
            row_copy(c, k, lax.rem(lon + k, NLON)).start()
            return 0

        lax.fori_loop(1, NLON, send_rows, 0)
        recv[c, lon] = sendbuf[c, lon]

    for k in range(BANDS + 1, 16):
        bands[k] = jnp.zeros((ROWS, COLS), F32)
    bands[BANDS] = labels[...].astype(F32)
    for c in range(CHUNKS):

        def wait_rows(k, _):
            row_arrival(c, lax.rem(lon + k, NLON)).wait_recv()
            return 0

        lax.fori_loop(1, NLON, wait_rows, 0)
        rows = recv[c].reshape(NLON * BUCKET, CW)
        blended = (dot(blend_hi, rows) + dot(blend_lo, rows)) / total
        blended = blended.astype(BF16).astype(F32)
        for b in range(CW // COLS):
            bands[c * (CW // COLS) + b] = blended[:, b * COLS : (b + 1) * COLS]

    pick_row = lax.broadcasted_iota(jnp.int32, (8, COLS), 0)
    pick_lane = lane_iota((8, COLS))
    pick = jnp.where(pick_lane == jnp.where(pick_row < 3, pick_row, pick_row + 122), 1.0, 0.0)
    columns = dot_nt(pick.astype(BF16), bands[...].reshape(16 * ROWS, COLS).astype(BF16))
    for k in range(16):
        picked[k] = jnp.concatenate(
            [columns[:, k * ROWS : (k + 1) * ROWS], jnp.zeros((8, 64), F32)], axis=1)
    for x in range(3):
        hsend[3 + x] = picked[:, x, :].astype(BF16)
        hsend[6 + x] = picked[:, 3 + x, :].astype(BF16)
    for r in range(3):
        hsend[r] = bands[:, r, :].astype(BF16)
        hsend[9 + r] = bands[:, ROWS - 3 + r, :].astype(BF16)

    def halo_copies():
        made = [
            (hsend.at[0:9], from_down, (up, lon)),
            (hsend.at[3:12], from_up, (down, lon)),
            (hsend.at[3:6], side.at[3], (lat, left)),
            (hsend.at[6:9], side.at[0], (lat, right)),
            (hsend.at[3:6], side.at[5], (up, left)),
            (hsend.at[6:9], side.at[2], (up, right)),
            (hsend.at[3:6], side.at[4], (down, left)),
            (hsend.at[6:9], side.at[1], (down, right)),
        ]
        return [
            pltpu.make_async_remote_copy(
                src_ref=s, dst_ref=d, send_sem=halo_send.at[n], recv_sem=halo_recv.at[n],
                device_id=who, device_id_type=MESH)
            for n, (s, d, who) in enumerate(made)
        ]

    copies = halo_copies()
    for copy in copies:
        copy.start()

    for r in range(ROWS):
        comp[3 + r] = bands[:, r, :].astype(BF16)

    for copy in copies:
        copy.wait_recv()

    has_up, has_down = lat > 0, lat < NLAT - 1
    has_left, has_right = lon > 0, lon < NLON - 1
    for r in range(3):
        comp[r] = jnp.where(has_up, from_up[6 + r].astype(F32), 0.0).astype(BF16)
        comp[67 + r] = jnp.where(has_down, from_down[r].astype(F32), 0.0).astype(BF16)
    tile_lane = lane_iota((16, 128))

    def joined(middle, above, below, inside):
        turned = pltpu.roll(middle.astype(F32), 3, 1)
        result = jnp.where((tile_lane >= 3) & (tile_lane < 67), turned, 0.0)
        top = pltpu.roll(above.astype(F32), 67, 1)
        result = jnp.where((tile_lane < 3) & has_up, top, result)
        bottom = pltpu.roll(below.astype(F32), 67, 1)
        result = jnp.where((tile_lane >= 67) & (tile_lane < 70) & has_down, bottom, result)
        if inside is not None:
            result = jnp.where(inside, result, 0.0)
        return result.astype(BF16)

    for x in range(3):
        strip[x] = joined(side[0, x], side[1, x], side[2, x], has_left)
        strip[7 + x] = joined(side[3, x], side[4, x], side[5, x], has_right)
    for x in range(2):
        strip[3 + x] = joined(hsend[3 + x], from_up[x], from_down[3 + x], None)
        strip[5 + x] = joined(hsend[7 + x], from_up[4 + x], from_down[7 + x], None)

    for copy in copies:
        copy.wait_send()

    def drain(k, _):
        peer = lax.rem(lon + k, NLON)
        req_copy(k, peer).wait_send()
        for c in range(CHUNKS):
            row_copy(c, k, peer).wait_send()
        return 0

    lax.fori_loop(1, NLON, drain, 0)


def gather(patches, requests, foot, widx, cw, labels):
    return pl.pallas_call(
        gather_kernel,
        out_shape=(
            jax.ShapeDtypeStruct((70, 16, 128), BF16),
            jax.ShapeDtypeStruct((10, 16, 128), BF16),
        ),
        in_specs=[VM, VM, VM, VM, pl.BlockSpec(memory_space=pltpu.SMEM), VM],
        out_specs=(VM, VM),
        scratch_shapes=[
            pltpu.VMEM((NLON, 1, 128), jnp.int32),
            pltpu.VMEM((STORE, NLON * BUCKET), BF16),
            pltpu.VMEM((CHUNKS, NLON, BUCKET, CW), BF16),
            pltpu.VMEM((CHUNKS, NLON, BUCKET, CW), BF16),
            pltpu.VMEM((16, ROWS, COLS), F32),
            pltpu.VMEM((16, 8, 128), F32),
            pltpu.VMEM((12, 16, 128), BF16),
            pltpu.VMEM((9, 16, 128), BF16),
            pltpu.VMEM((9, 16, 128), BF16),
            pltpu.VMEM((6, 3, 16, 128), BF16),
            pltpu.SemaphoreType.DMA((NLON,)),
            pltpu.SemaphoreType.DMA((NLON,)),
            pltpu.SemaphoreType.DMA((CHUNKS, NLON)),
            pltpu.SemaphoreType.DMA((CHUNKS, NLON)),
            pltpu.SemaphoreType.DMA((8,)),
            pltpu.SemaphoreType.DMA((8,)),
        ],
        compiler_params=pltpu.CompilerParams(collective_id=0, has_side_effects=True),
        name="gather_blend_halo",
    )(patches, requests, foot, widx, cw, labels)


def halves(h):
    return 1.0 + jnp.tanh(h)


def twice_slope(h, a):
    return a * (1.0 + h * (2.0 - a))


def tile_kernel(
    comp, strip, w1, w2, head, skip_out, grads,
    w1k, w2k, w2a, x1, x2, x3, own, fact1, buf1, buf2, buf3, cols, skip3, acc2, acc1, acch, accl,
):
    lat, lon = lax.axis_index("lat"), lax.axis_index("lon")
    has_up, has_down = lat > 0, lat < NLAT - 1
    has_left, has_right = lon > 0, lon < NLON - 1

    w1k[...] = jnp.zeros_like(w1k)
    for t in range(9):
        w1k[:, 16 * t : 16 * t + BANDS] = (w1[t].astype(F32).T * 0.5).astype(BF16)
        w2k[:, 64 * t : 64 * (t + 1)] = (w2[t].astype(F32) * 0.5).astype(BF16)
        w2a[:, 64 * t : 64 * (t + 1)] = (0.5 * w2[8 - t].astype(F32).T).astype(BF16)
    headp = jnp.concatenate(
        [head[...].astype(F32), jnp.zeros((16 - NCLASS, FEAT), F32)], axis=0)
    head_half = (0.5 * headp).astype(BF16)
    headp = headp.astype(BF16)

    def spread(dst, tile, index, left_col, right_col, lane_row, height):
        lanes = lane_iota((height, 128))
        put_left = pltpu.roll(left_col, lax.rem(128 - lane_row, 128), 1)
        put_right = pltpu.roll(right_col, lax.rem(255 - lane_row, 128), 1)
        dst[index, 0:height] = jnp.where(lanes == 0, put_left, pltpu.roll(tile, 1, 1))
        dst[index, height : 2 * height] = tile
        dst[index, 2 * height : 3 * height] = jnp.where(
            lanes == 127, put_right, pltpu.roll(tile, 127, 1))

    def wide(ref, first, count):
        return jnp.concatenate([ref[first + j] for j in range(count)], axis=1)

    def stack_of(ref, first, count):
        return jnp.concatenate([wide(ref, first + u, count) for u in (-1, 0, 1)], axis=0)

    comp_left = strip[2]
    comp_right = strip[7]

    def spread_comp(i, _):
        for j in range(7):
            t = i * 7 + j
            spread(x1, comp[t], t, comp_left, comp_right, t, 16)
        return 0

    lax.fori_loop(0, 10, spread_comp, 0)

    turned = [[pltpu.roll(strip[s], (128 - u) % 128, 1) for u in (-1, 0, 1)] for s in range(10)]
    lanes64 = lane_iota((FEAT, 128))
    row_ok = ((lanes64 >= 3) | has_up) & ((lanes64 < 67) | has_down) & (lanes64 >= 1) & (lanes64 < 69)
    beside = (1, 2, 3, 6, 7, 8)
    half = dot(w1k[...], jnp.concatenate(
        [jnp.concatenate([turned[s + v][u] for u in range(3) for v in (-1, 0, 1)], axis=0)
         for s in beside], axis=1))
    value = half * halves(half)
    for n, s in enumerate(beside):
        keep = row_ok
        if s in (1, 2):
            keep = keep & has_left
        if s in (7, 8):
            keep = keep & has_right
        cols[n] = jnp.where(keep, value[:, 128 * n : 128 * (n + 1)], 0.0).astype(BF16)

    half = jnp.concatenate(
        [dot(w1k[...], stack_of(x1, 1, 2)), dot(w1k[...], stack_of(x1, 67, 2))], axis=1)
    value = half * halves(half)
    for j, (index, inside) in enumerate(((0, has_up), (1, has_up), (66, has_down), (67, has_down))):
        tile = jnp.where(inside, value[:, 128 * j : 128 * (j + 1)], 0.0).astype(BF16)
        spread(x2, tile, index, cols[1], cols[4], index + 1, FEAT)

    buf1[...] = dot(w1k[...], stack_of(x1, 3, 8))

    def conv_one(i, _):
        first = i * 8
        left_col, right_col = cols[1], cols[4]
        for j in range(8):
            half = buf1[:, 128 * j : 128 * (j + 1)]
            a = halves(half)
            fact1[first + j] = twice_slope(half, a)
            tile = (half * a).astype(BF16)
            spread(x2, tile, first + 2 + j, left_col, right_col, first + 3 + j, FEAT)
        buf1[...] = dot(w1k[...], stack_of(x1, jnp.minimum(first + 11, 59), 8))
        return 0

    lax.fori_loop(0, 8, conv_one, 0)

    def head_of(half, label):
        width = half.shape[1]
        a = halves(half)
        skip = half * a
        skip_bf16 = skip.astype(BF16)
        logits = dot(headp, skip_bf16)
        classes = lax.broadcasted_iota(jnp.int32, (16, width), 0)
        power = jnp.where(classes < NCLASS, jnp.exp(logits), 0.0)
        total = jnp.sum(power, axis=0, keepdims=True)
        onehot = classes == label.astype(jnp.int32)
        error = (power * (1.0 / total) - jnp.where(onehot, 1.0, 0.0)).astype(BF16)
        slope = dot_tn(head_half, error) * twice_slope(half, a)
        loss = jnp.log(total) - jnp.sum(jnp.where(onehot, logits, 0.0), axis=0, keepdims=True)
        return skip, skip_bf16, error, slope, loss

    def label_row(tile):
        return tile.astype(F32)[BANDS : BANDS + 1, :]

    beside = [jnp.concatenate(
        [pltpu.roll(cols[middle + v], (128 - u) % 128, 1) for u in (-1, 0, 1) for v in (-1, 0, 1)],
        axis=0) for middle in (1, 4)]
    around = jnp.concatenate([stack_of(x2, 1, 1), stack_of(x2, 66, 1)] + beside, axis=1)
    edge_label = jnp.concatenate(
        [label_row(comp[2]), label_row(comp[67]), label_row(strip[2]), label_row(strip[7])], axis=1)
    _, _, _, edge_slope, _ = head_of(dot(w2k[...], around), edge_label)
    slope_left = jnp.where(row_ok & has_left, edge_slope[:, 256:384], 0.0).astype(BF16)
    slope_right = jnp.where(row_ok & has_right, edge_slope[:, 384:512], 0.0).astype(BF16)
    slope_top = jnp.where(has_up, edge_slope[:, 0:128], 0.0).astype(BF16)
    slope_bottom = jnp.where(has_down, edge_slope[:, 128:256], 0.0).astype(BF16)
    cols[0] = slope_left
    cols[2] = slope_right
    spread(x3, slope_top, 0, slope_left, slope_right, 2, FEAT)
    spread(x3, slope_bottom, 65, slope_left, slope_right, 67, FEAT)
    for index in (0, 1, 66, 67):
        own[index] = jnp.zeros((FEAT, 128), BF16)

    acc1[...] = jnp.zeros_like(acc1)
    acch[...] = jnp.zeros_like(acch)
    accl[...] = jnp.zeros_like(accl)
    buf2[...] = dot(w2k[...], stack_of(x2, 2, 8))

    def conv_two(i, _):
        first = i * 8
        left_col, right_col = cols[0], cols[2]
        heads = []
        for j in range(0, 8, 2):
            label = jnp.concatenate([label_row(comp[first + 3 + j + m]) for m in range(2)], axis=1)
            skip, skip_bf16, error, slope, loss = head_of(buf2[:, 128 * j : 128 * (j + 2)], label)
            heads.append((skip_bf16, error))
            accl[...] += loss
            for m in range(2):
                tile = slope[:, 128 * m : 128 * (m + 1)].astype(BF16)
                spread(x3, tile, first + 1 + j + m, left_col, right_col, first + 3 + j + m, FEAT)
                own[first + 2 + j + m] = tile
                skip3[:, j + m, :] = skip[:, 128 * m : 128 * (m + 1)]
        acch[...] += dot_nt(jnp.concatenate([h[0] for h in heads], axis=1),
                            jnp.concatenate([h[1] for h in heads], axis=1))
        skip_out[:, pl.ds(pl.multiple_of(first, 8), 8), :] = skip3[...].astype(BF16)
        buf2[...] = dot(w2k[...], stack_of(x2, jnp.minimum(first + 10, 58), 8))
        return 0

    lax.fori_loop(0, 8, conv_two, 0)

    def grad_two(first, count):
        lhs = jnp.concatenate([wide(own, first - u, count) for u in (-1, 0, 1)], axis=0)
        return dot_nt(lhs, wide(x2, first, count))

    acc2[...] = grad_two(1, 1) + grad_two(66, 1)
    buf3[...] = dot(w2a[...], stack_of(x3, 1, 8))

    def back_one(i, _):
        first = i * 8
        slopes = [(buf3[:, 128 * j : 128 * (j + 1)] * fact1[first + j]).astype(BF16)
                  for j in range(8)]
        acc1[...] += dot_nt(jnp.concatenate(slopes, axis=1), stack_of(x1, first + 3, 8))
        acc2[...] += grad_two(first + 2, 8)
        buf3[...] = dot(w2a[...], stack_of(x3, jnp.minimum(first + 9, 57), 8))
        return 0

    lax.fori_loop(0, 8, back_one, 0)

    loss_total = jnp.sum(jnp.sum(accl[...], axis=1, keepdims=True), axis=0, keepdims=True)
    packed = jnp.concatenate(
        [acc2[64 * u : 64 * (u + 1), :] for u in range(3)]
        + [acc1[...], acch[...], jnp.broadcast_to(loss_total, (FEAT, 32))], axis=1)
    for g in range(8):
        for h in range(6):
            grads[6 * g + h] = packed[8 * g : 8 * (g + 1), 128 * h : 128 * (h + 1)]


def tile_pass(comp, strip, w1, w2, head):
    return pl.pallas_call(
        tile_kernel,
        out_shape=(
            jax.ShapeDtypeStruct((FEAT, ROWS, COLS), BF16),
            jax.ShapeDtypeStruct((48, 8, 128), F32),
        ),
        in_specs=[VM] * 5,
        out_specs=(VM, VM),
        scratch_shapes=[
            pltpu.VMEM((64, 144), BF16),
            pltpu.VMEM((64, 576), BF16),
            pltpu.VMEM((64, 576), BF16),
            pltpu.VMEM((70, 48, 128), BF16),
            pltpu.VMEM((68, 192, 128), BF16),
            pltpu.VMEM((66, 192, 128), BF16),
            pltpu.VMEM((68, 64, 128), BF16),
            pltpu.VMEM((64, 64, 128), F32),
            pltpu.VMEM((64, 1024), F32),
            pltpu.VMEM((64, 1024), F32),
            pltpu.VMEM((64, 1024), F32),
            pltpu.VMEM((6, 64, 128), BF16),
            pltpu.VMEM((64, 8, 128), F32),
            pltpu.VMEM((192, 192), F32),
            pltpu.VMEM((64, 144), F32),
            pltpu.VMEM((64, 16), F32),
            pltpu.VMEM((1, 256), F32),
        ],
        name="tile_forward_backward",
    )(comp, strip, w1, w2, head)


def sum_kernel(part, out, first, second, whole, s1, r1, s2, r2, s3, r3):
    lat, lon = lax.axis_index("lat"), lax.axis_index("lon")
    barrier = pltpu.get_barrier_semaphore()

    def greet_lon(k, _):
        pl.semaphore_signal(
            barrier, inc=1, device_id=(lat, lax.rem(lon + k, NLON)), device_id_type=MESH)
        return 0

    def greet_lat(k, _):
        pl.semaphore_signal(
            barrier, inc=1, device_id=(lax.rem(lat + k, NLAT), lon), device_id_type=MESH)
        return 0

    lax.fori_loop(1, NLON, greet_lon, 0)
    lax.fori_loop(1, NLAT, greet_lat, 0)
    pl.semaphore_wait(barrier, NLON - 1 + NLAT - 1)

    def scatter(k, peer, source):
        return pltpu.make_async_remote_copy(
            src_ref=part.at[pl.ds(3 * peer, 3)], dst_ref=first.at[source],
            send_sem=s1.at[k], recv_sem=r1.at[source],
            device_id=(lat, peer), device_id_type=MESH)

    def start1(k, _):
        scatter(k, lax.rem(lon + k, NLON), lon).start()
        return 0

    def wait1(k, _):
        peer = lax.rem(lon + k, NLON)
        scatter(k, peer, peer).wait_recv()
        return 0

    lax.fori_loop(1, NLON, start1, 0)
    first[lon] = part[pl.ds(3 * lon, 3)]
    lax.fori_loop(1, NLON, wait1, 0)
    piece = first[0]
    for n in range(1, NLON):
        piece = piece + first[n]
    second[lat] = piece

    def exchange(k, peer, source):
        return pltpu.make_async_remote_copy(
            src_ref=second.at[lat], dst_ref=second.at[source],
            send_sem=s2.at[k], recv_sem=r2.at[source],
            device_id=(peer, lon), device_id_type=MESH)

    def start2(k, _):
        exchange(k, lax.rem(lat + k, NLAT), lat).start()
        return 0

    def wait2(k, _):
        peer = lax.rem(lat + k, NLAT)
        exchange(k, peer, peer).wait_recv()
        return 0

    lax.fori_loop(1, NLAT, start2, 0)
    lax.fori_loop(1, NLAT, wait2, 0)
    piece = second[0]
    for n in range(1, NLAT):
        piece = piece + second[n]
    whole[pl.ds(3 * lon, 3)] = piece * (1.0 / (512 * 2048))

    def spread(k, peer, source):
        return pltpu.make_async_remote_copy(
            src_ref=whole.at[pl.ds(3 * lon, 3)], dst_ref=whole.at[pl.ds(3 * source, 3)],
            send_sem=s3.at[k], recv_sem=r3.at[source],
            device_id=(lat, peer), device_id_type=MESH)

    def start3(k, _):
        spread(k, lax.rem(lon + k, NLON), lon).start()
        return 0

    def wait3(k, _):
        peer = lax.rem(lon + k, NLON)
        spread(k, peer, peer).wait_recv()
        return 0

    lax.fori_loop(1, NLON, start3, 0)
    lax.fori_loop(1, NLON, wait3, 0)
    out[...] = whole[...]

    def drain(k, _):
        scatter(k, lax.rem(lon + k, NLON), lon).wait_send()
        spread(k, lax.rem(lon + k, NLON), lon).wait_send()
        return 0

    def drain2(k, _):
        exchange(k, lax.rem(lat + k, NLAT), lat).wait_send()
        return 0

    lax.fori_loop(1, NLON, drain, 0)
    lax.fori_loop(1, NLAT, drain2, 0)


def summed(part):
    return pl.pallas_call(
        sum_kernel,
        out_shape=jax.ShapeDtypeStruct((48, 8, 128), F32),
        in_specs=[VM],
        out_specs=VM,
        scratch_shapes=[
            pltpu.VMEM((NLON, 3, 8, 128), F32),
            pltpu.VMEM((NLAT, 3, 8, 128), F32),
            pltpu.VMEM((48, 8, 128), F32),
            pltpu.SemaphoreType.DMA((NLON,)),
            pltpu.SemaphoreType.DMA((NLON,)),
            pltpu.SemaphoreType.DMA((NLAT,)),
            pltpu.SemaphoreType.DMA((NLAT,)),
            pltpu.SemaphoreType.DMA((NLON,)),
            pltpu.SemaphoreType.DMA((NLON,)),
        ],
        compiler_params=pltpu.CompilerParams(collective_id=1, has_side_effects=True),
        name="gradient_sum",
    )(part)


def unpack_kernel(whole, grad1, grad2, gradh, loss):
    packed = jnp.concatenate(
        [jnp.concatenate([whole[6 * g + h] for h in range(6)], axis=1) for g in range(8)], axis=0)
    packed_t = packed.T
    for t in range(9):
        grad2[t] = packed[:, 64 * t : 64 * (t + 1)]
        grad1[t] = packed_t[576 + 16 * t : 576 + 16 * t + BANDS, :]
    gradh[...] = packed_t[720 : 720 + NCLASS, :]
    loss[...] = packed[0:1, 736:737]


def unpacked(whole):
    return pl.pallas_call(
        unpack_kernel,
        out_shape=(
            jax.ShapeDtypeStruct((9, BANDS, FEAT), F32),
            jax.ShapeDtypeStruct((9, FEAT, FEAT), F32),
            jax.ShapeDtypeStruct((NCLASS, FEAT), F32),
            jax.ShapeDtypeStruct((1, 1), F32),
        ),
        in_specs=[VM],
        out_specs=(VM, VM, VM, VM),
        name="unpack",
    )(whole)


def body(patches, requests, foot, widx, cw, labels, w1, w2, head):
    comp, strip = gather(patches, requests, foot.T, widx.T, cw, labels)
    skip, part = tile_pass(comp, strip, jnp.swapaxes(w1, 1, 2), w2, head)
    grad1, grad2, gradh, loss = unpacked(summed(part))
    return skip, jnp.swapaxes(grad1, 1, 2), grad2, gradh, loss.reshape(())


def solution(mesh):
    placed = (
        P(("lat", "lon"), None),
        P("lat", "lon"),
        P("lat", "lon"),
        P("lat", "lon"),
        P(),
        P("lat", "lon"),
        P(),
        P(),
        P(),
    )
    return jax.shard_map(
        body,
        mesh=mesh,
        in_specs=placed,
        out_specs=(P(None, "lat", "lon"), P(), P(), P(), P()),
        check_vma=False,
    )
```

```python
import functools

import jax
import jax.numpy as jnp
from jax import lax
from jax.experimental import pallas as pl
from jax.experimental.pallas import tpu as pltpu
from jax.sharding import PartitionSpec as P

F32 = jnp.float32
BF16 = jnp.bfloat16
NLAT, NLON = 8, 16
ROWS, COLS, BANDS, FEAT, NCLASS, SLOTS, BUCKET, STORE = 64, 128, 12, 64, 11, 8, 32, 192
WIDTH = BANDS * COLS
CHUNKS = 3
CW = WIDTH // CHUNKS
MESH = pl.DeviceIdType.MESH
VM = pl.BlockSpec(memory_space=pltpu.VMEM)


def lane_iota(shape):
    return lax.broadcasted_iota(jnp.int32, shape, len(shape) - 1)


def dot_nt(a, b):
    return lax.dot_general(a, b, (((1,), (1,)), ((), ())), preferred_element_type=F32)


def dot_tn(a, b):
    return lax.dot_general(a, b, (((0,), (0,)), ((), ())), preferred_element_type=F32)


def dot(a, b):
    return jnp.dot(a, b, preferred_element_type=F32)


def gather_kernel(
    patches, requests, foot, widx, cw, labels, comp, strip,
    reqs, hot, sendbuf, recv, bands, picked, hsend, from_up, from_down, side,
    req_send, req_recv, row_send, row_recv, halo_send, halo_recv,
):
    lat, lon = lax.axis_index("lat"), lax.axis_index("lon")
    up, down = lax.rem(lat + NLAT - 1, NLAT), lax.rem(lat + 1, NLAT)
    left, right = lax.rem(lon + NLON - 1, NLON), lax.rem(lon + 1, NLON)

    barrier = pltpu.get_barrier_semaphore()

    def greet(k, _):
        peer = lax.rem(lon + k, NLON)
        pl.semaphore_signal(barrier, inc=1, device_id=(lat, peer), device_id_type=MESH)
        return 0

    lax.fori_loop(1, NLON, greet, 0)
    for i in (up, down):
        for d in (left, lon, right):
            pl.semaphore_signal(barrier, inc=1, device_id=(i, d), device_id_type=MESH)
    pl.semaphore_wait(barrier, NLON - 1 + 6)

    def req_copy(k, peer):
        start = pl.multiple_of((peer // 4) * 128, 128)
        return pltpu.make_async_remote_copy(
            src_ref=requests.at[:, pl.ds(start, 128)], dst_ref=reqs.at[lon],
            send_sem=req_send.at[k], recv_sem=req_recv.at[lon],
            device_id=(lat, peer), device_id_type=MESH)

    def req_arrival(source):
        return pltpu.make_async_remote_copy(
            src_ref=requests.at[:, pl.ds(0, 128)], dst_ref=reqs.at[source],
            send_sem=req_send.at[0], recv_sem=req_recv.at[source],
            device_id=(lat, lon), device_id_type=MESH)

    def send_req(k, _):
        req_copy(k, lax.rem(lon + k, NLON)).start()
        return 0

    lax.fori_loop(1, NLON, send_req, 0)
    own = pl.multiple_of((lon // 4) * 128, 128)
    reqs[lon] = requests[:, pl.ds(own, 128)]

    level = widx[...].astype(F32).T
    weight = jnp.zeros((ROWS, SLOTS), F32)
    for q in range(16):
        weight = jnp.where(level == q, cw[q], weight)
    entry = foot[...].astype(F32).T.astype(jnp.int32)
    weight = jnp.where(entry >= 0, weight, 0.0)
    total = jnp.sum(weight, axis=1, keepdims=True)
    position = lane_iota((ROWS, NLON * BUCKET))
    blend = jnp.zeros((ROWS, NLON * BUCKET), F32)
    for k in range(SLOTS):
        blend = blend + jnp.where(entry[:, k : k + 1] == position, weight[:, k : k + 1], 0.0)
    blend_hi = blend.astype(BF16)
    blend_lo = (blend - blend_hi.astype(F32)).astype(BF16)

    def wait_req(k, _):
        req_arrival(lax.rem(lon + k, NLON)).wait_recv()
        return 0

    lax.fori_loop(1, NLON, wait_req, 0)

    lanes = lane_iota((1, 128))
    base = 32 * lax.rem(lon, 4)
    store_row = lax.broadcasted_iota(jnp.int32, (STORE, 128), 0)
    for t in range(4):
        asked = jnp.zeros((1, 128), jnp.int32)
        for j in range(4):
            turned = pltpu.roll(reqs[4 * t + j], lax.rem(32 * j - base + 128, 128), 1)
            asked = jnp.where((lanes >= 32 * j) & (lanes < 32 * j + 32), turned, asked)
        hot[:, 128 * t : 128 * (t + 1)] = jnp.where(store_row == asked, 1.0, 0.0).astype(BF16)

    def row_copy(c, k, peer):
        return pltpu.make_async_remote_copy(
            src_ref=sendbuf.at[c, peer], dst_ref=recv.at[c, lon],
            send_sem=row_send.at[c, k], recv_sem=row_recv.at[c, lon],
            device_id=(lat, peer), device_id_type=MESH)

    def row_arrival(c, source):
        return pltpu.make_async_remote_copy(
            src_ref=sendbuf.at[c, source], dst_ref=recv.at[c, source],
            send_sem=row_send.at[c, 0], recv_sem=row_recv.at[c, source],
            device_id=(lat, lon), device_id_type=MESH)

    for c in range(CHUNKS):
        rows = dot_tn(hot[...], patches[:, c * CW : (c + 1) * CW]).astype(BF16)
        sendbuf[c] = rows.reshape(NLON, BUCKET, CW)

        def send_rows(k, _):
            row_copy(c, k, lax.rem(lon + k, NLON)).start()
            return 0

        lax.fori_loop(1, NLON, send_rows, 0)
        recv[c, lon] = sendbuf[c, lon]

    for k in range(BANDS + 1, 16):
        bands[k] = jnp.zeros((ROWS, COLS), F32)
    bands[BANDS] = labels[...].astype(F32)
    for c in range(CHUNKS):

        def wait_rows(k, _):
            row_arrival(c, lax.rem(lon + k, NLON)).wait_recv()
            return 0

        lax.fori_loop(1, NLON, wait_rows, 0)
        rows = recv[c].reshape(NLON * BUCKET, CW)
        blended = (dot(blend_hi, rows) + dot(blend_lo, rows)) / total
        blended = blended.astype(BF16).astype(F32)
        for b in range(CW // COLS):
            bands[c * (CW // COLS) + b] = blended[:, b * COLS : (b + 1) * COLS]

    pick_row = lax.broadcasted_iota(jnp.int32, (8, COLS), 0)
    pick_lane = lane_iota((8, COLS))
    pick = jnp.where(pick_lane == jnp.where(pick_row < 3, pick_row, pick_row + 122), 1.0, 0.0)
    columns = dot_nt(pick.astype(BF16), bands[...].reshape(16 * ROWS, COLS).astype(BF16))
    for k in range(16):
        picked[k] = jnp.concatenate(
            [columns[:, k * ROWS : (k + 1) * ROWS], jnp.zeros((8, 64), F32)], axis=1)
    for x in range(3):
        hsend[3 + x] = picked[:, x, :].astype(BF16)
        hsend[6 + x] = picked[:, 3 + x, :].astype(BF16)
    swap_out = lax.broadcasted_iota(jnp.int32, (128, 128), 0)
    swap = jnp.where((swap_out % 16) * 8 + swap_out // 16 == lane_iota((128, 128)), 1.0, 0.0)
    swap = swap.astype(BF16)

    def row_tiles(g):
        block = bands[:, 8 * g : 8 * g + 8, :].reshape(128, COLS).astype(BF16)
        return dot(swap, block).astype(BF16).reshape(8, 16, COLS)

    top, bottom = row_tiles(0), row_tiles(7)
    hsend[0:3] = top[0:3]
    hsend[9:12] = bottom[5:8]

    def halo_copies():
        made = [
            (hsend.at[0:9], from_down, (up, lon)),
            (hsend.at[3:12], from_up, (down, lon)),
            (hsend.at[3:6], side.at[3], (lat, left)),
            (hsend.at[6:9], side.at[0], (lat, right)),
            (hsend.at[3:6], side.at[5], (up, left)),
            (hsend.at[6:9], side.at[2], (up, right)),
            (hsend.at[3:6], side.at[4], (down, left)),
            (hsend.at[6:9], side.at[1], (down, right)),
        ]
        return [
            pltpu.make_async_remote_copy(
                src_ref=s, dst_ref=d, send_sem=halo_send.at[n], recv_sem=halo_recv.at[n],
                device_id=who, device_id_type=MESH)
            for n, (s, d, who) in enumerate(made)
        ]

    copies = halo_copies()
    for copy in copies:
        copy.start()

    comp[3:11] = top
    for g in range(1, 7):
        comp[3 + 8 * g : 11 + 8 * g] = row_tiles(g)
    comp[59:67] = bottom

    for copy in copies:
        copy.wait_recv()

    has_up, has_down = lat > 0, lat < NLAT - 1
    has_left, has_right = lon > 0, lon < NLON - 1
    for r in range(3):
        comp[r] = jnp.where(has_up, from_up[6 + r].astype(F32), 0.0).astype(BF16)
        comp[67 + r] = jnp.where(has_down, from_down[r].astype(F32), 0.0).astype(BF16)
    tile_lane = lane_iota((16, 128))

    def joined(middle, above, below, inside):
        turned = pltpu.roll(middle.astype(F32), 3, 1)
        result = jnp.where((tile_lane >= 3) & (tile_lane < 67), turned, 0.0)
        top = pltpu.roll(above.astype(F32), 67, 1)
        result = jnp.where((tile_lane < 3) & has_up, top, result)
        bottom = pltpu.roll(below.astype(F32), 67, 1)
        result = jnp.where((tile_lane >= 67) & (tile_lane < 70) & has_down, bottom, result)
        if inside is not None:
            result = jnp.where(inside, result, 0.0)
        return result.astype(BF16)

    for x in range(3):
        strip[x] = joined(side[0, x], side[1, x], side[2, x], has_left)
        strip[7 + x] = joined(side[3, x], side[4, x], side[5, x], has_right)
    for x in range(2):
        strip[3 + x] = joined(hsend[3 + x], from_up[x], from_down[3 + x], None)
        strip[5 + x] = joined(hsend[7 + x], from_up[4 + x], from_down[7 + x], None)

    for copy in copies:
        copy.wait_send()

    def drain(k, _):
        peer = lax.rem(lon + k, NLON)
        req_copy(k, peer).wait_send()
        for c in range(CHUNKS):
            row_copy(c, k, peer).wait_send()
        return 0

    lax.fori_loop(1, NLON, drain, 0)


def gather(patches, requests, foot, widx, cw, labels):
    return pl.pallas_call(
        gather_kernel,
        out_shape=(
            jax.ShapeDtypeStruct((70, 16, 128), BF16),
            jax.ShapeDtypeStruct((10, 16, 128), BF16),
        ),
        in_specs=[VM, VM, VM, VM, pl.BlockSpec(memory_space=pltpu.SMEM), VM],
        out_specs=(VM, VM),
        scratch_shapes=[
            pltpu.VMEM((NLON, 1, 128), jnp.int32),
            pltpu.VMEM((STORE, NLON * BUCKET), BF16),
            pltpu.VMEM((CHUNKS, NLON, BUCKET, CW), BF16),
            pltpu.VMEM((CHUNKS, NLON, BUCKET, CW), BF16),
            pltpu.VMEM((16, ROWS, COLS), F32),
            pltpu.VMEM((16, 8, 128), F32),
            pltpu.VMEM((12, 16, 128), BF16),
            pltpu.VMEM((9, 16, 128), BF16),
            pltpu.VMEM((9, 16, 128), BF16),
            pltpu.VMEM((6, 3, 16, 128), BF16),
            pltpu.SemaphoreType.DMA((NLON,)),
            pltpu.SemaphoreType.DMA((NLON,)),
            pltpu.SemaphoreType.DMA((CHUNKS, NLON)),
            pltpu.SemaphoreType.DMA((CHUNKS, NLON)),
            pltpu.SemaphoreType.DMA((8,)),
            pltpu.SemaphoreType.DMA((8,)),
        ],
        compiler_params=pltpu.CompilerParams(collective_id=0, has_side_effects=True),
        name="gather_blend_halo",
    )(patches, requests, foot, widx, cw, labels)


def halves(h):
    return 1.0 + jnp.tanh(h)


def twice_slope(h, a):
    return a * (1.0 + h * (2.0 - a))


def tile_kernel(
    comp, strip, w1, w2, head, skip_out, out_a, out_b,
    w1k, w2k, w2a, x1, x2, x3, fact1, buf1, buf2, buf3, cols, acc2, acc1, acch, accl,
    part_a, part_b, lat_a, lat_b, lon_a, lon_b, all_a, all_b,
    s1a, r1a, s1b, r1b, s2a, r2a, s2b, r2b, s3a, r3a, s3b, r3b,
):
    lat, lon = lax.axis_index("lat"), lax.axis_index("lon")
    barrier = pltpu.get_barrier_semaphore()

    def greet_lon(k, _):
        pl.semaphore_signal(
            barrier, inc=1, device_id=(lat, lax.rem(lon + k, NLON)), device_id_type=MESH)
        return 0

    def greet_lat(k, _):
        pl.semaphore_signal(
            barrier, inc=1, device_id=(lax.rem(lat + k, NLAT), lon), device_id_type=MESH)
        return 0

    lax.fori_loop(1, NLON, greet_lon, 0)
    lax.fori_loop(1, NLAT, greet_lat, 0)
    has_up, has_down = lat > 0, lat < NLAT - 1
    has_left, has_right = lon > 0, lon < NLON - 1

    w1k[...] = jnp.zeros_like(w1k)
    for t in range(9):
        w1k[:, 16 * t : 16 * t + BANDS] = (w1[t].astype(F32).T * 0.5).astype(BF16)
        w2k[:, 64 * t : 64 * (t + 1)] = (w2[t].astype(F32) * 0.5).astype(BF16)
        w2a[:, 64 * t : 64 * (t + 1)] = (0.5 * w2[8 - t].astype(F32).T).astype(BF16)
    headp = jnp.concatenate(
        [head[...].astype(F32), jnp.zeros((16 - NCLASS, FEAT), F32)], axis=0)
    head_half = (0.5 * headp).astype(BF16)
    headp = headp.astype(BF16)

    def spread(dst, tile, index, left_col, right_col, lane_row, height):
        lanes = lane_iota((height, 128))
        put_left = pltpu.roll(left_col, lax.rem(128 - lane_row, 128), 1)
        put_right = pltpu.roll(right_col, lax.rem(255 - lane_row, 128), 1)
        dst[index, 0:height] = jnp.where(lanes == 0, put_left, pltpu.roll(tile, 1, 1))
        dst[index, height : 2 * height] = tile
        dst[index, 2 * height : 3 * height] = jnp.where(
            lanes == 127, put_right, pltpu.roll(tile, 127, 1))

    def wide(ref, first, count):
        return jnp.concatenate([ref[first + j] for j in range(count)], axis=1)

    def stack_of(ref, first, count):
        return jnp.concatenate([wide(ref, first + u, count) for u in (-1, 0, 1)], axis=0)

    comp_left = strip[2]
    comp_right = strip[7]

    def spread_comp(i, _):
        for j in range(7):
            t = i * 7 + j
            spread(x1, comp[t], t, comp_left, comp_right, t, 16)
        return 0

    lax.fori_loop(0, 10, spread_comp, 0)

    turned = [[pltpu.roll(strip[s], (128 - u) % 128, 1) for u in (-1, 0, 1)] for s in range(10)]
    lanes64 = lane_iota((FEAT, 128))
    row_ok = ((lanes64 >= 3) | has_up) & ((lanes64 < 67) | has_down) & (lanes64 >= 1) & (lanes64 < 69)
    beside = (1, 2, 3, 6, 7, 8)
    half = dot(w1k[...], jnp.concatenate(
        [jnp.concatenate([turned[s + v][u] for u in range(3) for v in (-1, 0, 1)], axis=0)
         for s in beside], axis=1))
    value = half * halves(half)
    for n, s in enumerate(beside):
        keep = row_ok
        if s in (1, 2):
            keep = keep & has_left
        if s in (7, 8):
            keep = keep & has_right
        cols[n] = jnp.where(keep, value[:, 128 * n : 128 * (n + 1)], 0.0).astype(BF16)

    half = jnp.concatenate(
        [dot(w1k[...], stack_of(x1, 1, 2)), dot(w1k[...], stack_of(x1, 67, 2))], axis=1)
    value = half * halves(half)
    for j, (index, inside) in enumerate(((0, has_up), (1, has_up), (66, has_down), (67, has_down))):
        tile = jnp.where(inside, value[:, 128 * j : 128 * (j + 1)], 0.0).astype(BF16)
        spread(x2, tile, index, cols[1], cols[4], index + 1, FEAT)

    buf1[...] = dot(w1k[...], stack_of(x1, 3, 8))

    def conv_one(i, _):
        first = i * 8
        left_col, right_col = cols[1], cols[4]
        for j in range(8):
            half = buf1[:, 128 * j : 128 * (j + 1)]
            a = halves(half)
            fact1[first + j] = twice_slope(half, a)
            tile = (half * a).astype(BF16)
            spread(x2, tile, first + 2 + j, left_col, right_col, first + 3 + j, FEAT)
        buf1[...] = dot(w1k[...], stack_of(x1, jnp.minimum(first + 11, 59), 8))
        return 0

    lax.fori_loop(0, 8, conv_one, 0)

    def head_of(half, label):
        width = half.shape[1]
        a = halves(half)
        skip = (half * a).astype(BF16)
        logits = dot(headp, skip)
        classes = lax.broadcasted_iota(jnp.int32, (16, width), 0)
        power = jnp.where(classes < NCLASS, jnp.exp(logits), 0.0)
        total = jnp.sum(power, axis=0, keepdims=True)
        onehot = classes == label.astype(jnp.int32)
        error = (power * (1.0 / total) - jnp.where(onehot, 1.0, 0.0)).astype(BF16)
        slope = dot_tn(head_half, error) * twice_slope(half, a)
        loss = jnp.log(total) - jnp.sum(jnp.where(onehot, logits, 0.0), axis=0, keepdims=True)
        return skip, error, slope, loss

    def label_row(tile):
        return tile.astype(F32)[BANDS : BANDS + 1, :]

    beside = [jnp.concatenate(
        [pltpu.roll(cols[middle + v], (128 - u) % 128, 1) for u in (-1, 0, 1) for v in (-1, 0, 1)],
        axis=0) for middle in (1, 4)]
    around = jnp.concatenate([stack_of(x2, 1, 1), stack_of(x2, 66, 1)] + beside, axis=1)
    edge_label = jnp.concatenate(
        [label_row(comp[2]), label_row(comp[67]), label_row(strip[2]), label_row(strip[7])], axis=1)
    _, _, edge_slope, _ = head_of(dot(w2k[...], around), edge_label)
    slope_left = jnp.where(row_ok & has_left, edge_slope[:, 256:384], 0.0).astype(BF16)
    slope_right = jnp.where(row_ok & has_right, edge_slope[:, 384:512], 0.0).astype(BF16)
    slope_top = jnp.where(has_up, edge_slope[:, 0:128], 0.0).astype(BF16)
    slope_bottom = jnp.where(has_down, edge_slope[:, 128:256], 0.0).astype(BF16)
    cols[0] = slope_left
    cols[2] = slope_right
    spread(x3, slope_top, 0, slope_left, slope_right, 2, FEAT)
    spread(x3, slope_bottom, 65, slope_left, slope_right, 67, FEAT)

    swap_out = lax.broadcasted_iota(jnp.int32, (128, 128), 0)
    swap = jnp.where((swap_out % 8) * 16 + swap_out // 8 == lane_iota((128, 128)), 1.0, 0.0)
    swap = swap.astype(BF16)
    acc2[...] = jnp.zeros_like(acc2)
    acc1[...] = jnp.zeros_like(acc1)
    acch[...] = jnp.zeros_like(acch)
    accl[...] = jnp.zeros_like(accl)
    buf2[...] = dot(w2k[...], stack_of(x2, 2, 8))

    def conv_two(i, _):
        first = i * 8
        left_col, right_col = cols[0], cols[2]
        heads, slopes = [], []
        for j in range(0, 8, 2):
            label = jnp.concatenate([label_row(comp[first + 3 + j + m]) for m in range(2)], axis=1)
            skip, error, slope, loss = head_of(buf2[:, 128 * j : 128 * (j + 2)], label)
            heads.append((skip, error))
            accl[...] += loss
            for m in range(2):
                tile = slope[:, 128 * m : 128 * (m + 1)].astype(BF16)
                spread(x3, tile, first + 1 + j + m, left_col, right_col, first + 3 + j + m, FEAT)
                slopes.append(tile)
        acch[...] += dot_nt(jnp.concatenate([h[0] for h in heads], axis=1),
                            jnp.concatenate([h[1] for h in heads], axis=1))
        rows = [heads[j // 2][0][:, 128 * (j % 2) : 128 * (j % 2 + 1)] for j in range(8)]
        block = jnp.concatenate(
            [jnp.concatenate([row[16 * g : 16 * (g + 1)] for g in range(4)], axis=1) for row in rows],
            axis=0)
        block = dot(swap, block).astype(BF16)
        for g in range(4):
            skip_out[16 * g : 16 * (g + 1), pl.ds(pl.multiple_of(first, 8), 8), :] = (
                block[:, 128 * g : 128 * (g + 1)].reshape(16, 8, 128))
        acc2[...] += dot_nt(jnp.concatenate(slopes, axis=1), stack_of(x2, first + 2, 8))
        buf2[...] = dot(w2k[...], stack_of(x2, jnp.minimum(first + 10, 58), 8))
        return 0

    lax.fori_loop(0, 8, conv_two, 0)

    loss_total = jnp.sum(jnp.sum(accl[...], axis=1, keepdims=True), axis=0, keepdims=True)
    packed = jnp.concatenate(
        [acc2[...], acch[...], jnp.broadcast_to(loss_total, (FEAT, 48))], axis=1)
    for g in range(NLAT):
        part_a[g] = packed[8 * g : 8 * (g + 1), :]
    pl.semaphore_wait(barrier, NLON - 1 + NLAT - 1)

    def over_lat(k, part, land, send, recv, source):
        peer = lax.rem(lat + k, NLAT)
        return pltpu.make_async_remote_copy(
            src_ref=part.at[peer], dst_ref=land.at[source], send_sem=send.at[k],
            recv_sem=recv.at[source], device_id=(peer, lon), device_id_type=MESH)

    def over_lon(k, land, send, recv, source):
        return pltpu.make_async_remote_copy(
            src_ref=land.at[lon], dst_ref=land.at[source], send_sem=send.at[k],
            recv_sem=recv.at[source], device_id=(lat, lax.rem(lon + k, NLON)), device_id_type=MESH)

    def back_lat(k, land, send, recv, source):
        return pltpu.make_async_remote_copy(
            src_ref=land.at[lat], dst_ref=land.at[source], send_sem=send.at[k],
            recv_sem=recv.at[source], device_id=(lax.rem(lat + k, NLAT), lon), device_id_type=MESH)

    def each(count, do):
        def step(k, _):
            do(k)
            return 0

        lax.fori_loop(1, count, step, 0)

    each(NLAT, lambda k: over_lat(k, part_a, lat_a, s1a, r1a, lat).start())
    lat_a[lat] = part_a[lat]

    buf3[...] = dot(w2a[...], stack_of(x3, 1, 8))

    def back_one(i, _):
        first = i * 8
        slopes = [(buf3[:, 128 * j : 128 * (j + 1)] * fact1[first + j]).astype(BF16)
                  for j in range(8)]
        acc1[...] += dot_nt(jnp.concatenate(slopes, axis=1), stack_of(x1, first + 3, 8))
        buf3[...] = dot(w2a[...], stack_of(x3, jnp.minimum(first + 9, 57), 8))
        return 0

    lax.fori_loop(0, 8, back_one, 0)

    packed = jnp.concatenate([acc1[...], jnp.zeros((FEAT, 112), F32)], axis=1)
    for g in range(NLAT):
        part_b[g] = packed[8 * g : 8 * (g + 1), :]
    each(NLAT, lambda k: over_lat(k, part_b, lat_b, s1b, r1b, lat).start())
    lat_b[lat] = part_b[lat]

    def added(ref, count):
        result = ref[0]
        for n in range(1, count):
            result = result + ref[n]
        return result

    def lat_source(k):
        return lax.rem(lat + k, NLAT)

    def lon_source(k):
        return lax.rem(lon + k, NLON)

    each(NLAT, lambda k: over_lat(k, part_a, lat_a, s1a, r1a, lat_source(k)).wait_recv())
    lon_a[lon] = added(lat_a, NLAT)
    each(NLON, lambda k: over_lon(k, lon_a, s2a, r2a, lon).start())
    each(NLAT, lambda k: over_lat(k, part_b, lat_b, s1b, r1b, lat_source(k)).wait_recv())
    lon_b[lon] = added(lat_b, NLAT)
    each(NLON, lambda k: over_lon(k, lon_b, s2b, r2b, lon).start())
    each(NLON, lambda k: over_lon(k, lon_a, s2a, r2a, lon_source(k)).wait_recv())
    all_a[lat] = added(lon_a, NLON) * (1.0 / (512 * 2048))
    each(NLAT, lambda k: back_lat(k, all_a, s3a, r3a, lat).start())
    each(NLON, lambda k: over_lon(k, lon_b, s2b, r2b, lon_source(k)).wait_recv())
    all_b[lat] = added(lon_b, NLON) * (1.0 / (512 * 2048))
    each(NLAT, lambda k: back_lat(k, all_b, s3b, r3b, lat).start())
    each(NLAT, lambda k: back_lat(k, all_a, s3a, r3a, lat_source(k)).wait_recv())
    out_a[...] = all_a[...]
    each(NLAT, lambda k: back_lat(k, all_b, s3b, r3b, lat_source(k)).wait_recv())
    out_b[...] = all_b[...]

    def drain_lat(k):
        over_lat(k, part_a, lat_a, s1a, r1a, lat).wait_send()
        over_lat(k, part_b, lat_b, s1b, r1b, lat).wait_send()
        back_lat(k, all_a, s3a, r3a, lat).wait_send()
        back_lat(k, all_b, s3b, r3b, lat).wait_send()

    def drain_lon(k):
        over_lon(k, lon_a, s2a, r2a, lon).wait_send()
        over_lon(k, lon_b, s2b, r2b, lon).wait_send()

    each(NLAT, drain_lat)
    each(NLON, drain_lon)


def tile_pass(comp, strip, w1, w2, head):
    return pl.pallas_call(
        tile_kernel,
        out_shape=(
            jax.ShapeDtypeStruct((FEAT, ROWS, COLS), BF16),
            jax.ShapeDtypeStruct((NLAT, 8, 640), F32),
            jax.ShapeDtypeStruct((NLAT, 8, 256), F32),
        ),
        in_specs=[VM] * 5,
        out_specs=(VM, VM, VM),
        scratch_shapes=[
            pltpu.VMEM((64, 144), BF16),
            pltpu.VMEM((64, 576), BF16),
            pltpu.VMEM((64, 576), BF16),
            pltpu.VMEM((70, 48, 128), BF16),
            pltpu.VMEM((68, 192, 128), BF16),
            pltpu.VMEM((66, 192, 128), BF16),
            pltpu.VMEM((64, 64, 128), F32),
            pltpu.VMEM((64, 1024), F32),
            pltpu.VMEM((64, 1024), F32),
            pltpu.VMEM((64, 1024), F32),
            pltpu.VMEM((6, 64, 128), BF16),
            pltpu.VMEM((64, 576), F32),
            pltpu.VMEM((64, 144), F32),
            pltpu.VMEM((64, 16), F32),
            pltpu.VMEM((1, 256), F32),
            pltpu.VMEM((NLAT, 8, 640), F32),
            pltpu.VMEM((NLAT, 8, 256), F32),
            pltpu.VMEM((NLAT, 8, 640), F32),
            pltpu.VMEM((NLAT, 8, 256), F32),
            pltpu.VMEM((NLON, 8, 640), F32),
            pltpu.VMEM((NLON, 8, 256), F32),
            pltpu.VMEM((NLAT, 8, 640), F32),
            pltpu.VMEM((NLAT, 8, 256), F32),
        ]
        + [pltpu.SemaphoreType.DMA((NLAT,))] * 4
        + [pltpu.SemaphoreType.DMA((NLON,))] * 4
        + [pltpu.SemaphoreType.DMA((NLAT,))] * 4,
        compiler_params=pltpu.CompilerParams(collective_id=1, has_side_effects=True),
        name="tile_forward_backward_sum",
    )(comp, strip, w1, w2, head)


def unpack_kernel(whole_a, whole_b, grad1, grad2, gradh, loss):
    packed = jnp.concatenate([whole_a[g] for g in range(NLAT)], axis=0)
    first = jnp.concatenate([whole_b[g] for g in range(NLAT)], axis=0).T
    for t in range(9):
        grad2[t] = packed[:, 64 * t : 64 * (t + 1)]
        grad1[t] = first[16 * t : 16 * t + BANDS, :]
    gradh[...] = packed[:, 512:640].T[64 : 64 + NCLASS, :]
    loss[...] = packed[0:1, 592:593]


def unpacked(whole_a, whole_b):
    return pl.pallas_call(
        unpack_kernel,
        out_shape=(
            jax.ShapeDtypeStruct((9, BANDS, FEAT), F32),
            jax.ShapeDtypeStruct((9, FEAT, FEAT), F32),
            jax.ShapeDtypeStruct((NCLASS, FEAT), F32),
            jax.ShapeDtypeStruct((1, 1), F32),
        ),
        in_specs=[VM, VM],
        out_specs=(VM, VM, VM, VM),
        name="unpack",
    )(whole_a, whole_b)


def body(patches, requests, foot, widx, cw, labels, w1, w2, head):
    comp, strip = gather(patches, requests, foot.T, widx.T, cw, labels)
    skip, whole_a, whole_b = tile_pass(comp, strip, jnp.swapaxes(w1, 1, 2), w2, head)
    grad1, grad2, gradh, loss = unpacked(whole_a, whole_b)
    return skip, jnp.swapaxes(grad1, 1, 2), grad2, gradh, loss.reshape(())


def solution(mesh):
    placed = (
        P(("lat", "lon"), None),
        P("lat", "lon"),
        P("lat", "lon"),
        P("lat", "lon"),
        P(),
        P("lat", "lon"),
        P(),
        P(),
        P(),
    )
    return jax.shard_map(
        body,
        mesh=mesh,
        in_specs=placed,
        out_specs=(P(None, "lat", "lon"), P(), P(), P(), P()),
        check_vma=False,
    )
```
